1024 devices in a mesh: pipe: 8 (over z), ctx: 128 (over y, x, core).
Axes of the slice: x: 8, y: 8, z: 8, core: 2. Of those that a mesh axis runs over, the one named last changes fastest.
Arguments:
- queries: bfloat16 [8, 16384, 4096], P('pipe', 'ctx'), may hold values from -6 to 6
- stash: bfloat16 [8, 16384, 1024], P('pipe', 'ctx'), may hold values from -6 to 6
- grad_out: bfloat16 [8, 16384, 4096], P('pipe', 'ctx'), may hold values from -6 to 6
- lengths: int32 [32], replicated, may hold values from 1 to 513, 16384 in all
Outputs:
- grad_kv: bfloat16 [8, 16384, 1024], P('pipe', 'ctx')
The draws below stay inside these ranges and needn't reach their ends.
Inputs may be any that keep to these rules, and one draw needn't show every extreme that they name: The lengths sum to 16384; one document is exactly 513 long.
All inputs are finite; a program needn't handle non-finite values.
Results may differ from the reference program's by a relative error of at most 0.0059.
Values may be sent and summed in bfloat16 or wider, within the bound.
A program may use at most 32 MiB of HBM per device.

```python
import math
import jax
import jax.numpy as jnp
import numpy as np
from jax import lax

H = 32
KVH = 4
HD = 128
TOK_DEV = 128
REACH = 5
TOKENS = 16384
SECTIONS = 8
DOCS = 32
MOST = 513
N_PIPE = 8


def draw_pair(key):
    key_q = jax.random.fold_in(key, 101)
    key_k = jax.random.fold_in(key, 202)
    queries = jnp.clip(jax.random.normal(key_q, (SECTIONS, TOKENS, H * HD), jnp.float32), -5.0, 5.0)
    stash = jnp.clip(jax.random.normal(key_k, (SECTIONS, TOKENS, 2 * KVH * HD), jnp.float32), -5.0, 5.0)
    return (queries, stash)


def draw_queries(key, part):
    return draw_pair(key)[0].astype(jnp.bfloat16)


def draw_stash(key, part):
    return draw_pair(key)[1].astype(jnp.bfloat16)


def steps_of(rng, dims, split, least, high):
    level, own = 1.0, jax.random.fold_in(rng, 6)
    for dim, shards_of in split:
        draws = jnp.exp(jax.random.uniform(jax.random.fold_in(own, dim), (shards_of,), jnp.float32, least / len(split), high / len(split)))
        level = level * jnp.repeat(draws, dims[dim] // shards_of).reshape([-1 if axis == dim else 1 for axis in range(len(dims))])
    return level


def split_up(number_of, total, most, slope):
    portions = [(1 << 20) // math.isqrt(grade ** slope) + 1 for grade in range(2, number_of + 1)]
    spare, holding = total - most - (number_of - 1), [1] * (number_of - 1)
    while spare > 0:
        movable = [i for i in range(number_of - 1) if holding[i] < most]
        whole, budget = sum([portions[i] for i in movable]), spare
        for i in movable:
            more = min(most - holding[i], max(1, budget * portions[i] // whole), spare)
            holding[i] = holding[i] + more
            spare = spare - more
    return np.array([most] + holding)


def uneven_parts(stream_key, count, total, limit, slope):
    if count == 2:
        one = jax.random.randint(stream_key, (), max(1, total - limit), min(limit, total - 1) + 1)
        return jnp.stack([one, total - one])
    sizes = jnp.asarray(split_up(count, total, limit, slope), jnp.int32)
    twos = (count - 1) // 2
    giver, taker = sizes[1:1 + 2 * twos:2], sizes[2:2 + 2 * twos:2]
    slack = jnp.minimum(giver - 1, limit - taker)
    passed = jax.random.randint(jax.random.fold_in(stream_key, 1), (twos,), 0, 1 << 20) % (slack + 1)
    sizes = sizes.at[1:1 + 2 * twos:2].set(giver - passed).at[2:2 + 2 * twos:2].set(taker + passed)
    return sizes[jax.random.permutation(jax.random.fold_in(stream_key, 2), count)]


def noise(stream_key, shape, width, most, pieces=(), kind=jnp.bfloat16):
    entries = width * jax.random.normal(stream_key, shape, jnp.float32)
    if pieces:
        entries = entries * steps_of(stream_key, shape, pieces, -0.22, 0.18)
    return jnp.clip(entries, -most, most).astype(kind)


def setup_inputs(seed: int = 0) -> dict:
    keys = jax.random.split(jax.random.key(seed), 5)
    return {
        "queries": draw_queries(jax.random.fold_in(keys[4], 71), 0),
        "stash": draw_stash(jax.random.fold_in(keys[4], 71), 0),
        "grad_out": noise(keys[2], (SECTIONS, TOKENS, H * HD), 1.0, 6.0, ((0, 8), (1, 128))),
        "lengths": uneven_parts(keys[3], DOCS, TOKENS, MOST, 2).astype(jnp.int32),
    }


def segment_of(positions, lengths):
    doc_ends = jnp.cumsum(lengths)
    return jnp.sum((doc_ends[None, :] <= positions[:, None]).astype(jnp.int32), axis=1)


def block_grads(query_block, cotangent, key_block, value_block, query_pos, key_pos, query_seg, key_seg):
    score_scale = HD ** -0.5
    query_wide = query_block.astype(jnp.float32)
    cot_wide = cotangent.astype(jnp.float32)
    key_wide = key_block.astype(jnp.float32)
    value_wide = value_block.astype(jnp.float32)
    scores = jnp.einsum("rhgd,khd->hgrk", query_wide, key_wide) * score_scale
    allowed = (key_seg[None, :] == query_seg[:, None]) & (key_pos[None, :] <= query_pos[:, None]) & (key_pos[None, :] >= 0)
    scores = jnp.where(allowed, scores, -1e30)
    row_top = jnp.max(scores, axis=-1, keepdims=True)
    raw_weights = jnp.exp(scores - row_top)
    weights = raw_weights / jnp.sum(raw_weights, axis=-1, keepdims=True)
    weights16 = weights.astype(jnp.bfloat16).astype(jnp.float32)
    output = jnp.einsum("hgrk,khd->rhgd", weights16, value_wide)
    row_delta = jnp.sum(cot_wide * output, axis=-1)
    dweights = jnp.einsum("rhgd,khd->hgrk", cot_wide, value_wide)
    dscores = weights * (dweights - jnp.transpose(row_delta, (1, 2, 0))[..., None]) * score_scale
    dscores = dscores.astype(jnp.bfloat16).astype(jnp.float32)
    grad_key = jnp.einsum("hgrk,rhgd->khd", dscores, query_wide)
    grad_value = jnp.einsum("hgrk,rhgd->khd", weights16, cot_wide)
    return grad_key, grad_value


def section_grads(section_queries, section_kv, section_cot, lengths):
    blocks = TOKENS // TOK_DEV
    group = H // KVH
    query_all = section_queries.reshape(blocks, TOK_DEV, KVH, group, HD)
    cot_all = section_cot.reshape(blocks, TOK_DEV, KVH, group, HD)
    kv_all = section_kv.reshape(blocks, TOK_DEV, 2, KVH, HD)
    padded = jnp.concatenate([jnp.zeros((REACH - 1, TOK_DEV, 2, KVH, HD), kv_all.dtype), kv_all], axis=0)
    joined = jnp.stack([padded[r:r + blocks] for r in range(REACH)], axis=1).reshape(blocks, REACH * TOK_DEV, 2, KVH, HD)

    def per_block(block_items):
        block_index, query_block, cotangent, kv_block = block_items
        first_row = block_index * TOK_DEV
        key_pos = first_row - (REACH - 1) * TOK_DEV + jnp.arange(REACH * TOK_DEV, dtype=jnp.int32)
        key_seg = segment_of(key_pos, lengths)
        tail = (REACH - 1) * TOK_DEV
        return block_grads(query_block, cotangent, kv_block[:, 0], kv_block[:, 1], key_pos[tail:], key_pos, key_seg[tail:], key_seg)

    grad_key, grad_value = lax.map(per_block, (jnp.arange(blocks, dtype=jnp.int32), query_all, cot_all, joined))
    key_grads = jnp.stack([grad_key, grad_value], axis=2).reshape(blocks, REACH, TOK_DEV, 2, KVH, HD)
    total = jnp.zeros((blocks, TOK_DEV, 2, KVH, HD), jnp.float32)
    for back in range(REACH):
        contrib = key_grads[:, REACH - 1 - back]
        if back > 0:
            contrib = jnp.concatenate([contrib[back:], jnp.zeros_like(contrib[:back])], axis=0)
        total = total + contrib
    return total.astype(jnp.bfloat16).reshape(TOKENS, 2 * KVH * HD)


def reference(queries, stash, grad_out, lengths):
    mirror = jnp.bitwise_xor(jnp.arange(N_PIPE, dtype=jnp.int32), N_PIPE // 2)
    held_kv = stash[mirror]

    def per_section(section_items):
        return section_grads(section_items[0], section_items[1], section_items[2], lengths)

    return lax.map(per_section, (queries, held_kv, grad_out))
```

```python
import functools
import math

import jax
import jax.numpy as jnp
from jax import lax
from jax.experimental import pallas as pl
from jax.experimental.pallas import tpu as pltpu
from jax.sharding import PartitionSpec as P

MESH = pl.DeviceIdType.MESH
H = 32
KVH = 4
HD = 128
GROUP = H // KVH
ROWS = 128
TEAM = 4
OVER = 32
SPAN = TEAM * ROWS + 2 * OVER
RIGHT = SPAN - OVER
PAIR = 2 * ROWS
SCALE = HD**-0.5
LOG2E = math.log2(math.e)
FAR = 1 << 20


def block_rows(s):
    return pl.ds(OVER + s * ROWS, ROWS)


def dot_nt(a, b):
    return lax.dot_general(a, b, (((1,), (1,)), ((), ())), preferred_element_type=jnp.float32)


def dot_nn(a, b):
    return lax.dot_general(a, b, (((1,), (0,)), ((), ())), preferred_element_type=jnp.float32)


def add_terms(key, value, query, cot, lo, hi, acc, diag):
    rows = key.shape[0]
    raw = dot_nt(key, query)
    dprobs = dot_nt(value, cot)
    pos = lax.broadcasted_iota(jnp.int32, (rows, PAIR), 0)
    raw = jnp.where((pos >= lo) & (pos <= hi), raw, -1e30)
    top = jnp.maximum(jnp.max(raw, axis=0, keepdims=True), -1e29)
    weights = jnp.exp2((raw - top) * (SCALE * LOG2E))
    total = jnp.sum(weights, axis=0, keepdims=True)
    probs = weights * (1.0 / jnp.where(total > 0.0, total, 1.0))
    probs16 = probs.astype(jnp.bfloat16)
    delta = jnp.sum(probs16.astype(jnp.float32) * dprobs, axis=0, keepdims=True)
    dscores = (probs * (dprobs - delta) * SCALE).astype(jnp.bfloat16)
    acc[0, pl.ds(0, rows)] += dot_nn(dscores, query)
    acc[1, pl.ds(0, rows)] += dot_nn(probs16, cot)


def kernel(
    n_pipe, n_ctx, lengths, queries, stash, grad_out, out,
    mine, kv, q_own, c_own, q_over, c_over, acc, own, terms, got, got_left, got_right,
    load_sem, bulk_sem, zs, zr, fs, fr, os, orr, gs, gr, gl, gh,
):
    z, c = lax.axis_index("pipe"), lax.axis_index("ctx")
    team, j = c // TEAM, c % TEAM
    first = team * TEAM
    has_left, has_right = team > 0, team < n_ctx // TEAM - 1
    partner = (z ^ (n_pipe // 2), c)

    def at(offset):
        return (z, first + offset)

    def stash_loads():
        for h in range(KVH):
            for t in range(2):
                yield pltpu.make_async_copy(
                    stash.at[0, :, pl.ds((t * KVH + h) * HD, HD)], mine.at[h, t], load_sem.at[2 * h + t]
                )

    for copy in stash_loads():
        copy.start()

    barrier = pltpu.get_barrier_semaphore()

    def greet(device):
        pl.semaphore_signal(barrier, inc=1, device_id=device, device_id_type=MESH)

    greet(partner)
    for step in range(1, TEAM):
        greet(at((j + step) % TEAM))

    @pl.when(has_left)
    def _():
        greet(at(-1))

    @pl.when(has_left & (j == 0))
    def _():
        greet(at(-2))

    @pl.when(has_right & (j == 2))
    def _():
        greet(at(TEAM))

    @pl.when(has_right & (j == 3))
    def _():
        for other in range(TEAM):
            greet(at(TEAM + other))

    for head in range(H):
        columns = pl.ds(head * HD, HD)
        pltpu.make_async_copy(queries.at[0, :, columns], q_own.at[head], bulk_sem.at[0]).start()
        pltpu.make_async_copy(grad_out.at[0, :, columns], c_own.at[head], bulk_sem.at[1]).start()

    def prefix(i, carry):
        size = lengths[i]
        start, stop = carry
        return (start + jnp.where(i < team, size, 0), stop + jnp.where(i <= team, size, 0))

    base = first * ROWS - OVER
    start, stop = lax.fori_loop(0, lengths.shape[0], prefix, (jnp.int32(0), jnp.int32(0)))
    start, stop = start - base, stop - base

    @pl.when(jnp.logical_not(has_left))
    def _():
        for h in range(KVH):
            for t in range(2):
                kv[h, t, pl.ds(0, OVER), :] = jnp.zeros((OVER, HD), jnp.bfloat16)

    for copy in stash_loads():
        copy.wait()
    expected = 4 + jnp.where(has_left, jnp.where(j == 0, 2, 1), 0)
    expected += jnp.where(has_right, jnp.where(j == 2, 1, jnp.where(j == 3, 4, 0)), 0)
    pl.semaphore_wait(barrier, expected)

    def to_partner(h, t):
        return pltpu.make_async_remote_copy(
            mine.at[h, t], kv.at[h, t, pl.ds(OVER + j * ROWS, ROWS)], zs.at[2 * h + t], zr.at[2 * h + t],
            device_id=partner, device_id_type=MESH,
        )

    for h in range(KVH):
        for t in range(2):
            to_partner(h, t).start()

    pltpu.make_async_copy(q_own, q_own, bulk_sem.at[0]).wait()
    pltpu.make_async_copy(c_own, c_own, bulk_sem.at[1]).wait()

    def over_queries(device):
        head_rows = pl.ds(0, OVER)
        return [
            pltpu.make_async_remote_copy(
                own_ref.at[:, head_rows, :], over_ref, os.at[i], orr.at[i], device_id=device, device_id_type=MESH
            )
            for i, (own_ref, over_ref) in enumerate(((q_own, q_over), (c_own, c_over)))
        ]

    @pl.when(has_left & (j == 0))
    def _():
        for copy in over_queries(at(-2)):
            copy.start()

    def role(me):
        used = OVER + (me + 1) * ROWS

        near = {0: (3, 2, 1), 1: (3, 2), 2: (3,), 3: ()}[me]

        def forward(h, t, n, rows, there, device, slot):
            return pltpu.make_async_remote_copy(
                kv.at[h, t, rows], kv.at[h, t, there], fs.at[n, 2 * h + t], fr.at[slot, 2 * h + t],
                device_id=device, device_id_type=MESH,
            )

        def forwards(h, t, act):
            for n, other in enumerate(near):
                act(forward(h, t, n, block_rows(me), block_rows(me), at(other), me))
            if me == 0:

                @pl.when(has_left)
                def _():
                    act(forward(h, t, 3, pl.ds(OVER, OVER), pl.ds(RIGHT, OVER), at(-2), 5))

            if me == 3:

                @pl.when(has_right)
                def _():
                    act(forward(h, t, 0, block_rows(3), block_rows(3), at(2), 3))
                    for other in range(TEAM):
                        act(forward(h, t, 1 + other, pl.ds(RIGHT - OVER, OVER), pl.ds(0, OVER), at(TEAM + other), 4))

        def arrive(h, t):
            pltpu.make_async_remote_copy(
                mine.at[h, t], kv.at[h, t, block_rows(me)], zs.at[2 * h + t], zr.at[2 * h + t],
                device_id=partner, device_id_type=MESH,
            ).wait_recv()
            forwards(h, t, lambda copy: copy.start())

        def arrived(h, t, rows, slot):
            forward(h, t, 0, rows, rows, partner, slot).wait_recv()

        def term(h, n, rows, there, device, recv):
            return pltpu.make_async_remote_copy(
                terms.at[h, :, rows], there, gs.at[n, h], recv, device_id=device, device_id_type=MESH
            )

        def sent_terms(h, act):
            for s in range(me):
                act(term(h, s, block_rows(s), got.at[me - 1, h], at(s), gr.at[me - 1, h]))

            @pl.when(has_left)
            def _():
                act(term(h, 3, pl.ds(0, OVER), got_left.at[me, h], at(-1), gl.at[me, h]))

            if me == 2:

                @pl.when(has_right)
                def _():
                    act(term(h, 2, block_rows(3), got.at[1, h], at(3), gr.at[1, h]))
                    act(term(h, 4, pl.ds(RIGHT, OVER), got_right.at[h], at(TEAM), gh.at[h]))

        column = lax.broadcasted_iota(jnp.int32, (1, PAIR), 1)
        hi = OVER + me * ROWS + column % ROWS
        lo = jnp.where(hi >= stop, stop, jnp.where(hi >= start, start, FAR))

        def compute(h):
            for t in range(2):
                for s in range(me):
                    arrived(h, t, block_rows(s), s)

                @pl.when(has_left)
                def _():
                    arrived(h, t, pl.ds(0, OVER), 4)

            acc[...] = jnp.zeros_like(acc)

            def pair(p, _):
                heads = pl.ds(h * GROUP + 2 * p, 2)
                add_terms(
                    kv[h, 0, pl.ds(0, used)], kv[h, 1, pl.ds(0, used)],
                    q_own[heads].reshape(PAIR, HD), c_own[heads].reshape(PAIR, HD), lo, hi, acc, me,
                )
                return 0

            lax.fori_loop(0, GROUP // 2, pair, 0)
            if me == 2:

                @pl.when(has_right)
                def _():
                    for t in range(2):
                        arrived(h, t, block_rows(3), 3)
                        arrived(h, t, pl.ds(RIGHT, OVER), 5)
                    heads = pl.ds(h * GROUP, GROUP)
                    hi_over = RIGHT + column % OVER
                    lo_over = jnp.where(hi_over < stop, start, FAR)
                    add_terms(
                        kv[h, 0], kv[h, 1], q_over[heads].reshape(PAIR, HD), c_over[heads].reshape(PAIR, HD),
                        lo_over, hi_over, acc, 4,
                    )

            own[h] = acc[:, OVER + me * ROWS : OVER + (me + 1) * ROWS, :]
            terms[h] = acc[...].astype(jnp.bfloat16)
            sent_terms(h, lambda copy: copy.start())

        for t in range(2):
            arrive(0, t)
        if me == 2:

            @pl.when(has_right)
            def _():
                for copy in over_queries(at(TEAM)):
                    copy.wait_recv()

        def head_step(h, _):
            @pl.when(h < KVH - 1)
            def _():
                for t in range(2):
                    arrive(h + 1, t)

            compute(h)
            return 0

        lax.fori_loop(0, KVH, head_step, 0)

        for h in range(KVH):
            total = own[h]
            sources = {0: (1, 2, 3), 1: (2, 3), 2: (3,), 3: ()}[me]
            for source in sources:
                term(h, 0, block_rows(me), got.at[source - 1, h], partner, gr.at[source - 1, h]).wait_recv()
                total = total + got[source - 1, h].astype(jnp.float32)
            own[h] = total
            if me == 0:

                @pl.when(has_left)
                def _():
                    term(h, 0, pl.ds(0, OVER), got_right.at[h], partner, gh.at[h]).wait_recv()
                    own[h, :, pl.ds(0, OVER)] += got_right[h].astype(jnp.float32)

            if me == 3:

                @pl.when(has_right)
                def _():
                    term(h, 0, block_rows(me), got.at[1, h], partner, gr.at[1, h]).wait_recv()
                    own[h] += got[1, h].astype(jnp.float32)
                    for other in range(TEAM):
                        term(h, 0, pl.ds(0, OVER), got_left.at[other, h], partner, gl.at[other, h]).wait_recv()
                        own[h, :, pl.ds(ROWS - OVER, OVER)] += got_left[other, h].astype(jnp.float32)

            for t in range(2):
                out[0, :, (t * KVH + h) * HD : (t * KVH + h + 1) * HD] = own[h, t].astype(jnp.bfloat16)

        for h in range(KVH):
            for t in range(2):
                to_partner(h, t).wait_send()
                forwards(h, t, lambda copy: copy.wait_send())
            sent_terms(h, lambda copy: copy.wait_send())
        if me == 0:

            @pl.when(has_left)
            def _():
                for copy in over_queries(at(-2)):
                    copy.wait_send()

    for me in range(TEAM):
        pl.when(j == me)(functools.partial(role, me))


def on_device(n_pipe, n_ctx, queries, stash, grad_out, lengths):
    bf16, f32 = jnp.bfloat16, jnp.float32
    dma = pltpu.SemaphoreType.DMA
    anywhere = pl.BlockSpec(memory_space=pl.ANY)
    return pl.pallas_call(
        functools.partial(kernel, n_pipe, n_ctx),
        out_shape=jax.ShapeDtypeStruct((1, ROWS, 2 * KVH * HD), bf16),
        in_specs=[pl.BlockSpec(memory_space=pltpu.SMEM), anywhere, anywhere, anywhere],
        out_specs=pl.BlockSpec(memory_space=pltpu.VMEM),
        scratch_shapes=[
            pltpu.VMEM((KVH, 2, ROWS, HD), bf16),
            pltpu.VMEM((KVH, 2, SPAN, HD), bf16),
            pltpu.VMEM((H, ROWS, HD), bf16),
            pltpu.VMEM((H, ROWS, HD), bf16),
            pltpu.VMEM((H, OVER, HD), bf16),
            pltpu.VMEM((H, OVER, HD), bf16),
            pltpu.VMEM((2, SPAN, HD), f32),
            pltpu.VMEM((KVH, 2, ROWS, HD), f32),
            pltpu.VMEM((KVH, 2, SPAN, HD), bf16),
            pltpu.VMEM((TEAM - 1, KVH, 2, ROWS, HD), bf16),
            pltpu.VMEM((TEAM, KVH, 2, OVER, HD), bf16),
            pltpu.VMEM((KVH, 2, OVER, HD), bf16),
            dma((2 * KVH,)), dma((2,)), dma((2 * KVH,)), dma((2 * KVH,)), dma((5, 2 * KVH)), dma((6, 2 * KVH)),
            dma((2,)), dma((2,)), dma((5, KVH)), dma((3, KVH)), dma((TEAM, KVH)), dma((KVH,)),
        ],
        compiler_params=pltpu.CompilerParams(collective_id=0, has_side_effects=True, vmem_limit_bytes=48 << 20),
        name="document_backward",
    )(lengths, queries, stash, grad_out)


def solution(mesh):
    placed = (P("pipe", "ctx", None), P("pipe", "ctx", None), P("pipe", "ctx", None), P())
    body = functools.partial(on_device, mesh.shape["pipe"], mesh.shape["ctx"])
    return jax.shard_map(body, mesh=mesh, in_specs=placed, out_specs=P("pipe", "ctx", None), check_vma=False)
```

```python
import functools
import math

import jax
import jax.numpy as jnp
from jax import lax
from jax.experimental import pallas as pl
from jax.experimental.pallas import tpu as pltpu
from jax.sharding import PartitionSpec as P

MESH = pl.DeviceIdType.MESH
H = 32
KVH = 4
HD = 128
GROUP = H // KVH
ROWS = 128
TEAM = 4
OVER = 32
SPAN = TEAM * ROWS + 2 * OVER
RIGHT = SPAN - OVER
PAIR = 2 * ROWS
SCALE = HD**-0.5
LOG2E = math.log2(math.e)
FAR = 1 << 20
NEVER = -1e30


def block_rows(s):
    return pl.ds(OVER + s * ROWS, ROWS)


def dot_nt(a, b):
    return lax.dot_general(a, b, (((1,), (1,)), ((), ())), preferred_element_type=jnp.float32)


def dot_nn(a, b):
    return lax.dot_general(a, b, (((1,), (0,)), ((), ())), preferred_element_type=jnp.float32)


def keep(rows, first, lo, hi, raw):
    pos = first + lax.broadcasted_iota(jnp.int32, (rows, PAIR), 0)
    ok = pos >= lo if hi is None else pos <= hi if lo is None else (pos >= lo) & (pos <= hi)
    return jnp.where(ok, raw, NEVER)


def pieces_of(own_first, own_rows, cut=None):
    edge = min(2 * OVER, own_first)
    cuts = [(0, edge), (edge, cut or own_first), (cut or own_first, own_first), (own_first, own_first + own_rows)]
    return [(first, last - first) for first, last in cuts if last > first]


def scores_of(key, value, query, cot, pieces):
    return [
        (dot_nt(key(first, rows), query), dot_nt(value(first, rows), cot)) for first, rows in pieces
    ]


def add_terms(scored, query, cot, pieces, lo, hi, any_lo, acc, fresh):
    raws, tops = [], []
    own_first = pieces[-1][0]
    here = None if any_lo is None else lo < own_first
    for (first, rows), (raw, _) in zip(pieces, scored):
        if first == own_first:
            raw = keep(rows, first, lo if any_lo is not None or own_first < 2 * OVER else None, hi, raw)
        elif first == 0:
            raw = keep(rows, first, lo, None, raw)
        top = jnp.max(raw, axis=0, keepdims=True)
        if any_lo is not None and 0 < first < own_first:
            top = jnp.where(here, top, NEVER)
        raws.append(raw)
        tops.append(top)
    top = jnp.maximum(functools.reduce(jnp.maximum, tops), -1e29)
    middle = top if any_lo is None else jnp.where(here, top, -NEVER)
    weights, total, delta = [], 0.0, 0.0
    for (first, _), raw, (_, dprobs) in zip(pieces, raws, scored):
        weight = jnp.exp2((raw - (middle if 0 < first < own_first else top)) * (SCALE * LOG2E))
        weights.append(weight)
        total += jnp.sum(weight, axis=0, keepdims=True)
        delta += jnp.sum(weight * dprobs, axis=0, keepdims=True)
    inverse = 1.0 / jnp.where(total > 0.0, total, 1.0)
    delta = delta * inverse
    for (first, rows), weight, (_, dprobs) in zip(pieces, weights, scored):
        probs = weight * inverse
        dscores = (probs * (dprobs - delta)).astype(jnp.bfloat16)
        for t, term in enumerate((dot_nn(dscores, query), dot_nn(probs.astype(jnp.bfloat16), cot))):
            rows_here = pl.ds(first, rows)
            acc[t, rows_here] = term if first >= fresh else acc[t, rows_here] + term


def kernel(
    n_pipe, n_ctx, lengths, queries, stash, grad_out, out,
    mine, kv, q_own, c_own, q_over, c_over, acc, terms, got, got_left, got_right,
    load_sem, bulk_sem, zs, zr, fs, fr, os, orr, gs, gr, gl, gh, ts, tr,
):
    z, c = lax.axis_index("pipe"), lax.axis_index("ctx")
    team, j = c // TEAM, c % TEAM
    first = team * TEAM
    has_left, has_right = team > 0, team < n_ctx // TEAM - 1
    partner = (z ^ (n_pipe // 2), c)

    def at(offset):
        return (z, first + offset)

    barrier = pltpu.get_barrier_semaphore()

    def greet(device):
        pl.semaphore_signal(barrier, inc=1, device_id=device, device_id_type=MESH)

    greet(partner)

    def stash_load(h, t):
        return pltpu.make_async_copy(
            stash.at[0, :, pl.ds((t * KVH + h) * HD, HD)], mine.at[h, t], load_sem.at[2 * h + t]
        )

    for h in range(KVH):
        for t in range(2):
            stash_load(h, t).start()
    for step in range(1, TEAM):
        greet(at((j + step) % TEAM))

    @pl.when(has_left & (j % 2 == 0))
    def _():
        greet((partner[0], first - 1))

    @pl.when(has_left & (j == 0))
    def _():
        greet(at(-2))

    @pl.when(has_right & (j == 2))
    def _():
        greet(at(TEAM))

    @pl.when(has_right & (j == 3))
    def _():
        for other in range(TEAM):
            greet(at(TEAM + other))

    expected = 4 + jnp.where(has_left, jnp.where(j == 0, 2, 1), 0)
    expected += jnp.where(has_right, jnp.where(j == 2, 1, jnp.where(j == 3, 2, 0)), 0)
    pl.semaphore_wait(barrier, expected)

    def to_partner(h, t):
        return pltpu.make_async_remote_copy(
            mine.at[h, t], kv.at[h, t, pl.ds(OVER + j * ROWS, ROWS)], zs.at[2 * h + t], zr.at[2 * h + t],
            device_id=partner, device_id_type=MESH,
        )

    def tails_to(n):
        return pltpu.make_async_remote_copy(
            mine.at[:, :, pl.ds(ROWS - OVER, OVER), :], kv.at[:, :, pl.ds(0, OVER), :], ts.at[n], tr.at[0],
            device_id=(partner[0], first + TEAM + 2 * n), device_id_type=MESH,
        )

    @pl.when(has_right & (j == TEAM - 1))
    def _():
        for h in range(KVH):
            for t in range(2):
                stash_load(h, t).wait()
        for n in range(2):
            tails_to(1 - n).start()

    for h in range(KVH):
        for t in range(2):

            @pl.when(jnp.logical_not(has_right & (j == TEAM - 1)))
            def _():
                stash_load(h, t).wait()

            to_partner(h, t).start()

    def load_head(head, _):
        columns = pl.ds(pl.multiple_of(head * HD, HD), HD)
        pltpu.make_async_copy(queries.at[0, :, columns], q_own.at[head], bulk_sem.at[0]).start()
        pltpu.make_async_copy(grad_out.at[0, :, columns], c_own.at[head], bulk_sem.at[1]).start()
        return 0

    lax.fori_loop(0, H, load_head, 0)

    def prefix(i, carry):
        size = lengths[i]
        start, stop = carry
        return (start + jnp.where(i < team, size, 0), stop + jnp.where(i <= team, size, 0))

    base = first * ROWS - OVER
    start, stop = lax.fori_loop(0, lengths.shape[0], prefix, (jnp.int32(0), jnp.int32(0)))
    start, stop = start - base, stop - base

    @pl.when(jnp.logical_not(has_left) & (j % 2 == 0))
    def _():
        for h in range(KVH):
            for t in range(2):
                kv[h, t, pl.ds(0, OVER), :] = jnp.zeros((OVER, HD), jnp.bfloat16)

    pltpu.make_async_copy(q_own, q_own, bulk_sem.at[0]).wait()
    pltpu.make_async_copy(c_own, c_own, bulk_sem.at[1]).wait()

    def over_queries(device):
        head_rows = pl.ds(0, OVER)
        return [
            pltpu.make_async_remote_copy(
                own_ref.at[:, head_rows, :], over_ref, os.at[i], orr.at[i], device_id=device, device_id_type=MESH
            )
            for i, (own_ref, over_ref) in enumerate(((q_own, q_over), (c_own, c_over)))
        ]

    @pl.when(has_left & (j == 0))
    def _():
        for copy in over_queries(at(-2)):
            copy.start()

    def role(me):
        mate = me ^ 1
        edge = pl.ds(0, OVER + ROWS)
        tail_rows, head_rows = pl.ds(0, OVER), pl.ds(RIGHT, OVER)

        def pass_on(h, t, rows, there, device, n, slot):
            return pltpu.make_async_remote_copy(
                kv.at[h, t, rows], kv.at[h, t, there], fs.at[n, 2 * h + t], fr.at[slot, 2 * h + t],
                device_id=device, device_id_type=MESH,
            )

        def forwards(h, t, act):
            mine_rows = block_rows(me)
            if me < 2:
                act(pass_on(h, t, mine_rows, mine_rows, at(me + 2), 0, 1))
            if me == 0:

                @pl.when(has_left)
                def _():
                    act(pass_on(h, t, pl.ds(OVER, OVER), head_rows, at(-2), 2, 3))

            if me == 2:
                act(pass_on(h, t, mine_rows, mine_rows, at(3), 0, 0))
            if me == 3:

                act(pass_on(h, t, mine_rows, mine_rows, at(2), 0, 0))

        def relay(h, t):
            rows = block_rows(1) if me == 3 else edge
            return pass_on(h, t, rows, rows, at(mate), 1, 2)

        def arrive(h):
            for t in range(2):
                to_partner(h, t).wait_recv()
                forwards(h, t, lambda copy: copy.start())

        def arrived(h, t, rows, slot):
            pass_on(h, t, rows, rows, partner, 0, slot).wait_recv()

        def hand_over(h):
            if me % 2 == 0:

                @pl.when(has_left & (h == 0))
                def _():
                    tails_to(0).wait_recv()

            for t in range(2):
                if me >= 2:
                    arrived(h, t, block_rows(me - 2), 1)
                if me != 1:
                    relay(h, t).start()

        def term(src, dst, n, h, recv, device):
            return pltpu.make_async_remote_copy(src, dst, gs.at[n, h], recv, device_id=device, device_id_type=MESH)

        def returns(h, act):
            for s in range(me):
                act(term(terms.at[h, :, block_rows(s)], got.at[me - 1, h], s, h, gr.at[me - 1, h], at(s)))

            @pl.when(has_left)
            def _():
                act(term(terms.at[h, :, tail_rows], got_left.at[me, h], 3, h, gl.at[me, h], at(-1)))

            if me == 2:

                @pl.when(has_right)
                def _():
                    act(term(terms.at[h, :, block_rows(3)], got.at[1, h], 2, h, gr.at[1, h], at(3)))
                    act(term(terms.at[h, :, head_rows], got_right.at[h], 4, h, gh.at[h], at(TEAM)))

        column = lax.broadcasted_iota(jnp.int32, (1, PAIR), 1)
        hi = OVER + me * ROWS + column % ROWS
        lo = jnp.where(hi >= stop, stop, jnp.where(hi >= start, start, FAR))
        hi_over = RIGHT + column % OVER
        lo_over = jnp.where(hi_over < stop, start, FAR)
        used = OVER + (me + 1) * ROWS
        pieces = pieces_of(OVER + me * ROWS, ROWS)
        pieces_over = pieces_of(RIGHT, OVER, used)

        def compute(h):
            if me == 1:
                for t in range(2):
                    arrived(h, t, edge, 2)
            if me == 2:
                for t in range(2):
                    arrived(h, t, block_rows(1), 2)
                    arrived(h, t, block_rows(3), 0)

                @pl.when(has_right)
                def _():
                    for t in range(2):
                        arrived(h, t, head_rows, 3)

            if me == 3:
                for t in range(2):
                    arrived(h, t, edge, 2)
                    arrived(h, t, block_rows(2), 0)

            def key(first, rows):
                return kv[h, 0, pl.ds(first, rows)]

            def value(first, rows):
                return kv[h, 1, pl.ds(first, rows)]

            def operands(p):
                heads = pl.ds(h * GROUP + 2 * p, 2)
                return q_own[heads].reshape(PAIR, HD), c_own[heads].reshape(PAIR, HD)

            jobs = [(*operands(p), pieces, lo, hi, True if me in (0, 3) else None, 0 if p == 0 else SPAN) for p in range(4)]
            if me == 2:
                heads = pl.ds(h * GROUP, GROUP)
                query, cot = q_over[heads].reshape(PAIR, HD), c_over[heads].reshape(PAIR, HD)
                jobs.append((query, cot, pieces_over, lo_over, hi_over, True, used))
            scored = scores_of(key, value, *jobs[0][:3])
            for p, (query, cot, some, low, high, any_lo, fresh) in enumerate(jobs):
                after = scores_of(key, value, *jobs[p + 1][:3]) if p + 1 < len(jobs) else None
                add_terms(scored, query, cot, some, low, high, any_lo, acc.at[h], fresh)
                scored = after

            sent = [(0, OVER + me * ROWS)] + ([(used, SPAN - used)] if me == 2 else [])
            for first, rows in sent:
                terms[h, 0, pl.ds(first, rows)] = (acc[h, 0, pl.ds(first, rows)] * SCALE).astype(jnp.bfloat16)
                terms[h, 1, pl.ds(first, rows)] = acc[h, 1, pl.ds(first, rows)].astype(jnp.bfloat16)
            returns(h, lambda copy: copy.start())

        for h in range(2):
            arrive(h)
        if me == 2:

            @pl.when(has_right)
            def _():
                for copy in over_queries(at(TEAM)):
                    copy.wait_recv()

            @pl.when(jnp.logical_not(has_right))
            def _():
                q_over[...] = jnp.zeros_like(q_over)
                c_over[...] = jnp.zeros_like(c_over)
                for h in range(KVH):
                    for t in range(2):
                        kv[h, t, head_rows, :] = jnp.zeros((OVER, HD), jnp.bfloat16)

        hand_over(0)

        def head_step(h, _):
            @pl.when(h < KVH - 2)
            def _():
                arrive(h + 2)

            @pl.when(h < KVH - 1)
            def _():
                hand_over(h + 1)

            compute(h)
            return 0

        lax.fori_loop(0, KVH, head_step, 0)

        def finish(h, _):
            rows = block_rows(me)
            acc[h, 0, rows] = acc[h, 0, rows] * SCALE

            def add(src, recv, there):
                term(src, src, 0, h, recv, partner).wait_recv()
                acc[h, :, there] += src[...].astype(jnp.float32)

            for source in range(me + 1, TEAM):
                add(got.at[source - 1, h], gr.at[source - 1, h], rows)
            if me == 0:

                @pl.when(has_left)
                def _():
                    add(got_right.at[h], gh.at[h], pl.ds(OVER, OVER))

            if me == 3:

                @pl.when(has_right)
                def _():
                    add(got.at[1, h], gr.at[1, h], rows)
                    for other in range(TEAM):
                        add(got_left.at[other, h], gl.at[other, h], pl.ds(RIGHT - OVER, OVER))

            for t in range(2):
                columns = pl.ds(pl.multiple_of((t * KVH + h) * HD, HD), HD)
                out[0, :, columns] = acc[h, t, rows].astype(jnp.bfloat16)
            return 0

        lax.fori_loop(0, KVH, finish, 0)

        def drain(h, _):
            for t in range(2):
                to_partner(h, t).wait_send()
                forwards(h, t, lambda copy: copy.wait_send())
                if me != 1:
                    relay(h, t).wait_send()
            returns(h, lambda copy: copy.wait_send())
            return 0

        lax.fori_loop(0, KVH, drain, 0)
        if me == 0:

            @pl.when(has_left)
            def _():
                for copy in over_queries(at(-2)):
                    copy.wait_send()

        if me == 3:

            @pl.when(has_right)
            def _():
                for n in range(2):
                    tails_to(n).wait_send()

    for me in range(TEAM):
        pl.when(j == me)(functools.partial(role, me))


def on_device(n_pipe, n_ctx, queries, stash, grad_out, lengths):
    bf16, f32 = jnp.bfloat16, jnp.float32
    dma = pltpu.SemaphoreType.DMA
    anywhere = pl.BlockSpec(memory_space=pl.ANY)
    return pl.pallas_call(
        functools.partial(kernel, n_pipe, n_ctx),
        out_shape=jax.ShapeDtypeStruct((1, ROWS, 2 * KVH * HD), bf16),
        in_specs=[pl.BlockSpec(memory_space=pltpu.SMEM), anywhere, anywhere, anywhere],
        out_specs=pl.BlockSpec(memory_space=pltpu.VMEM),
        scratch_shapes=[
            pltpu.VMEM((KVH, 2, ROWS, HD), bf16),
            pltpu.VMEM((KVH, 2, SPAN, HD), bf16),
            pltpu.VMEM((H, ROWS, HD), bf16),
            pltpu.VMEM((H, ROWS, HD), bf16),
            pltpu.VMEM((H, OVER, HD), bf16),
            pltpu.VMEM((H, OVER, HD), bf16),
            pltpu.VMEM((KVH, 2, SPAN, HD), f32),
            pltpu.VMEM((KVH, 2, SPAN, HD), bf16),
            pltpu.VMEM((TEAM - 1, KVH, 2, ROWS, HD), bf16),
            pltpu.VMEM((TEAM, KVH, 2, OVER, HD), bf16),
            pltpu.VMEM((KVH, 2, OVER, HD), bf16),
            dma((2 * KVH,)), dma((2,)), dma((2 * KVH,)), dma((2 * KVH,)), dma((3, 2 * KVH)), dma((4, 2 * KVH)),
            dma((2,)), dma((2,)), dma((5, KVH)), dma((3, KVH)), dma((TEAM, KVH)), dma((KVH,)), dma((2,)), dma((1,)),
        ],
        compiler_params=pltpu.CompilerParams(
            collective_id=0, has_side_effects=True, vmem_limit_bytes=67043328,
        ),
        name="document_backward",
    )(lengths, queries, stash, grad_out)


def solution(mesh):
    placed = (P("pipe", "ctx", None), P("pipe", "ctx", None), P("pipe", "ctx", None), P())
    body = functools.partial(on_device, mesh.shape["pipe"], mesh.shape["ctx"])
    return jax.shard_map(body, mesh=mesh, in_specs=placed, out_specs=P("pipe", "ctx", None), check_vma=False)
```

```python
import functools
import math

import jax
import jax.numpy as jnp
from jax import lax
from jax.experimental import pallas as pl
from jax.experimental.pallas import tpu as pltpu
from jax.sharding import PartitionSpec as P

MESH = pl.DeviceIdType.MESH
H = 32
KVH = 4
HD = 128
GROUP = H // KVH
ROWS = 128
TEAM = 4
OVER = 32
SPAN = TEAM * ROWS + 2 * OVER
RIGHT = SPAN - OVER
PAIR = 2 * ROWS
SCALE = HD**-0.5
LOG2E = math.log2(math.e)
FAR = 1 << 20
NEVER = -1e30


def block_rows(s):
    return pl.ds(OVER + s * ROWS, ROWS)


def dot_nt(a, b):
    return lax.dot_general(a, b, (((1,), (1,)), ((), ())), preferred_element_type=jnp.float32)


def dot_nn(a, b):
    return lax.dot_general(a, b, (((1,), (0,)), ((), ())), preferred_element_type=jnp.float32)


def keep(rows, first, lo, hi, raw):
    pos = first + lax.broadcasted_iota(jnp.int32, (rows, PAIR), 0)
    ok = pos >= lo if hi is None else pos <= hi if lo is None else (pos >= lo) & (pos <= hi)
    return jnp.where(ok, raw, NEVER)


def pieces_of(own_first, own_rows, cut=None):
    edge = min(2 * OVER, own_first)
    cuts = [(0, edge), (edge, cut or own_first), (cut or own_first, own_first), (own_first, own_first + own_rows)]
    return [(first, last - first) for first, last in cuts if last > first]


def scores_of(key, value, query, cot, pieces):
    return [
        (dot_nt(key(first, rows), query), dot_nt(value(first, rows), cot)) for first, rows in pieces
    ]


def add_terms(scored, query, cot, pieces, lo, hi, any_lo, acc, fresh):
    raws, tops = [], []
    own_first = pieces[-1][0]
    here = None if any_lo is None else lo < own_first
    for (first, rows), (raw, _) in zip(pieces, scored):
        if first == own_first:
            raw = keep(rows, first, lo if any_lo is not None or own_first < 2 * OVER else None, hi, raw)
        elif first == 0:
            raw = keep(rows, first, lo, None, raw)
        top = jnp.max(raw, axis=0, keepdims=True)
        if any_lo is not None and 0 < first < own_first:
            top = jnp.where(here, top, NEVER)
        raws.append(raw)
        tops.append(top)
    top = jnp.maximum(functools.reduce(jnp.maximum, tops), -1e29)
    middle = top if any_lo is None else jnp.where(here, top, -NEVER)
    weights, total, delta = [], 0.0, 0.0
    for (first, _), raw, (_, dprobs) in zip(pieces, raws, scored):
        weight = jnp.exp2((raw - (middle if 0 < first < own_first else top)) * (SCALE * LOG2E))
        weights.append(weight)
        total += jnp.sum(weight, axis=0, keepdims=True)
        delta += jnp.sum(weight * dprobs, axis=0, keepdims=True)
    inverse = 1.0 / jnp.where(total > 0.0, total, 1.0)
    delta = delta * inverse
    for (first, rows), weight, (_, dprobs) in zip(pieces, weights, scored):
        probs = weight * inverse
        dscores = (probs * (dprobs - delta)).astype(jnp.bfloat16)
        for t, term in enumerate((dot_nn(dscores, query), dot_nn(probs.astype(jnp.bfloat16), cot))):
            rows_here = pl.ds(first, rows)
            acc[t, rows_here] = term if first >= fresh else acc[t, rows_here] + term


def kernel(
    n_pipe, n_ctx, lengths, queries, stash, grad_out, out,
    mine, kv, q_own, c_own, q_over, c_over, acc, terms, got, got_left, got_right,
    load_sem, bulk_sem, zs, zr, fs, fr, os, orr, gs, gr, gl, gh, ts, tr,
):
    z, c = lax.axis_index("pipe"), lax.axis_index("ctx")
    team, j = c // TEAM, c % TEAM
    first = team * TEAM
    has_left, has_right = team > 0, team < n_ctx // TEAM - 1
    partner = (z ^ (n_pipe // 2), c)

    def at(offset):
        return (z, first + offset)

    barrier = pltpu.get_barrier_semaphore()

    def greet(device):
        pl.semaphore_signal(barrier, inc=1, device_id=device, device_id_type=MESH)

    greet(partner)

    def stash_load(h, t):
        return pltpu.make_async_copy(
            stash.at[0, :, pl.ds((t * KVH + h) * HD, HD)], mine.at[h, t], load_sem.at[2 * h + t]
        )

    for h in range(KVH):
        for t in range(2):
            stash_load(h, t).start()
    for step in range(1, TEAM):
        greet(at((j + step) % TEAM))

    @pl.when(has_left & (j % 2 == 0))
    def _():
        greet((partner[0], first - 1))

    @pl.when(has_left & (j == 0))
    def _():
        greet(at(-2))

    @pl.when(has_right & (j == 2))
    def _():
        greet(at(TEAM))

    @pl.when(has_right & (j == 3))
    def _():
        for other in range(TEAM):
            greet(at(TEAM + other))

    expected = 4 + jnp.where(has_left, jnp.where(j == 0, 2, 1), 0)
    expected += jnp.where(has_right, jnp.where(j == 2, 1, jnp.where(j == 3, 2, 0)), 0)
    pl.semaphore_wait(barrier, expected)

    def to_partner(h, t):
        return pltpu.make_async_remote_copy(
            mine.at[h, t], kv.at[h, t, pl.ds(OVER + j * ROWS, ROWS)], zs.at[2 * h + t], zr.at[2 * h + t],
            device_id=partner, device_id_type=MESH,
        )

    def tails_to(n):
        return pltpu.make_async_remote_copy(
            mine.at[:, :, pl.ds(ROWS - OVER, OVER), :], kv.at[:, :, pl.ds(0, OVER), :], ts.at[n], tr.at[0],
            device_id=(partner[0], first + TEAM + 2 * n), device_id_type=MESH,
        )

    @pl.when(has_right & (j == TEAM - 1))
    def _():
        for h in range(KVH):
            for t in range(2):
                stash_load(h, t).wait()
        for n in range(2):
            tails_to(1 - n).start()

    for h in range(KVH):
        for t in range(2):

            @pl.when(jnp.logical_not(has_right & (j == TEAM - 1)))
            def _():
                stash_load(h, t).wait()

            to_partner(h, t).start()

    def load_head(head, _):
        columns = pl.ds(pl.multiple_of(head * HD, HD), HD)
        pltpu.make_async_copy(queries.at[0, :, columns], q_own.at[head], bulk_sem.at[0]).start()
        pltpu.make_async_copy(grad_out.at[0, :, columns], c_own.at[head], bulk_sem.at[1]).start()
        return 0

    lax.fori_loop(0, H, load_head, 0)

    def prefix(i, carry):
        size = lengths[i]
        start, stop = carry
        return (start + jnp.where(i < team, size, 0), stop + jnp.where(i <= team, size, 0))

    base = first * ROWS - OVER
    start, stop = lax.fori_loop(0, lengths.shape[0], prefix, (jnp.int32(0), jnp.int32(0)))
    start, stop = start - base, stop - base

    @pl.when(jnp.logical_not(has_left))
    def _():
        for h in range(KVH):
            for t in range(2):
                kv[h, t, pl.ds(0, OVER), :] = jnp.zeros((OVER, HD), jnp.bfloat16)

    pltpu.make_async_copy(q_own, q_own, bulk_sem.at[0]).wait()
    pltpu.make_async_copy(c_own, c_own, bulk_sem.at[1]).wait()

    def over_queries(device):
        head_rows = pl.ds(0, OVER)
        return [
            pltpu.make_async_remote_copy(
                own_ref.at[:, head_rows, :], over_ref, os.at[i], orr.at[i], device_id=device, device_id_type=MESH
            )
            for i, (own_ref, over_ref) in enumerate(((q_own, q_over), (c_own, c_over)))
        ]

    @pl.when(has_left & (j == 0))
    def _():
        for copy in over_queries(at(-2)):
            copy.start()

    def role(me):
        mate = me ^ 1
        tail_rows, head_rows = pl.ds(0, OVER), pl.ds(RIGHT, OVER)

        def pass_on(h, t, rows, there, device, n, slot):
            return pltpu.make_async_remote_copy(
                kv.at[h, t, rows], kv.at[h, t, there], fs.at[n, 2 * h + t], fr.at[slot, 2 * h + t],
                device_id=device, device_id_type=MESH,
            )

        def forwards(h, t, act):
            mine_rows = block_rows(me)
            for n, other in enumerate({0: (3, 2, 1), 1: (2, 3), 2: (3,), 3: (2,)}[me]):
                act(pass_on(h, t, mine_rows, mine_rows, at(other), n, me))
            if me == 0:

                @pl.when(has_left)
                def _():
                    act(pass_on(h, t, pl.ds(OVER, OVER), head_rows, at(-2), 3, 4))

        def tails_on():
            tails = kv.at[:, :, tail_rows, :]
            return pltpu.make_async_remote_copy(
                tails, tails, ts.at[0], tr.at[1], device_id=at(mate), device_id_type=MESH
            )

        def arrive(h):
            for t in range(2):
                to_partner(h, t).wait_recv()
                forwards(h, t, lambda copy: copy.start())

        def arrived(h, t, rows, slot):
            pass_on(h, t, rows, rows, partner, 0, slot).wait_recv()

        def term(src, dst, n, h, recv, device):
            return pltpu.make_async_remote_copy(src, dst, gs.at[n, h], recv, device_id=device, device_id_type=MESH)

        def returns(h, act):
            for s in range(me):
                act(term(terms.at[h, :, block_rows(s)], got.at[me - 1, h], s, h, gr.at[me - 1, h], at(s)))

            @pl.when(has_left)
            def _():
                act(term(terms.at[h, :, tail_rows], got_left.at[me, h], 3, h, gl.at[me, h], at(-1)))

            if me == 2:

                @pl.when(has_right)
                def _():
                    act(term(terms.at[h, :, block_rows(3)], got.at[1, h], 2, h, gr.at[1, h], at(3)))
                    act(term(terms.at[h, :, head_rows], got_right.at[h], 4, h, gh.at[h], at(TEAM)))

        column = lax.broadcasted_iota(jnp.int32, (1, PAIR), 1)
        hi = OVER + me * ROWS + column % ROWS
        lo = jnp.where(hi >= stop, stop, jnp.where(hi >= start, start, FAR))
        hi_over = RIGHT + column % OVER
        lo_over = jnp.where(hi_over < stop, start, FAR)
        used = OVER + (me + 1) * ROWS
        pieces = pieces_of(OVER + me * ROWS, ROWS)
        pieces_over = pieces_of(RIGHT, OVER, used)

        def compute(h):
            for t in range(2):
                for s in range(me):
                    arrived(h, t, block_rows(s), s)
                if me == 2:
                    arrived(h, t, block_rows(3), 3)

                    @pl.when(has_right)
                    def _():
                        arrived(h, t, head_rows, 4)

            def key(first, rows):
                return kv[h, 0, pl.ds(first, rows)]

            def value(first, rows):
                return kv[h, 1, pl.ds(first, rows)]

            def operands(p):
                heads = pl.ds(h * GROUP + 2 * p, 2)
                return q_own[heads].reshape(PAIR, HD), c_own[heads].reshape(PAIR, HD)

            jobs = [(*operands(p), pieces, lo, hi, True if me in (0, 3) else None, 0 if p == 0 else SPAN) for p in range(4)]
            if me == 2:
                heads = pl.ds(h * GROUP, GROUP)
                query, cot = q_over[heads].reshape(PAIR, HD), c_over[heads].reshape(PAIR, HD)
                jobs.append((query, cot, pieces_over, lo_over, hi_over, True, used))
            scored = scores_of(key, value, *jobs[0][:3])
            for p, (query, cot, some, low, high, any_lo, fresh) in enumerate(jobs):
                after = scores_of(key, value, *jobs[p + 1][:3]) if p + 1 < len(jobs) else None
                add_terms(scored, query, cot, some, low, high, any_lo, acc.at[h], fresh)
                scored = after

            sent = [(0, OVER + me * ROWS)] + ([(used, SPAN - used)] if me == 2 else [])
            for first, rows in sent:
                terms[h, 0, pl.ds(first, rows)] = (acc[h, 0, pl.ds(first, rows)] * SCALE).astype(jnp.bfloat16)
                terms[h, 1, pl.ds(first, rows)] = acc[h, 1, pl.ds(first, rows)].astype(jnp.bfloat16)
            returns(h, lambda copy: copy.start())

        ahead = KVH if me < 2 else 2
        for h in range(ahead):
            arrive(h)
        if me == 2:

            @pl.when(has_right)
            def _():
                for copy in over_queries(at(TEAM)):
                    copy.wait_recv()

            @pl.when(jnp.logical_not(has_right))
            def _():
                q_over[...] = jnp.zeros_like(q_over)
                c_over[...] = jnp.zeros_like(c_over)
                for h in range(KVH):
                    for t in range(2):
                        kv[h, t, head_rows, :] = jnp.zeros((OVER, HD), jnp.bfloat16)

        @pl.when(has_left)
        def _():
            if me % 2 == 0:
                tails_to(0).wait_recv()
                tails_on().start()
            else:
                tails_on().wait_recv()

        def head_step(h, _):
            if me >= 2:

                @pl.when(h < KVH - ahead)
                def _():
                    arrive(h + ahead)

            compute(h)
            return 0

        lax.fori_loop(0, KVH, head_step, 0)

        def finish(h, _):
            rows = block_rows(me)
            acc[h, 0, rows] = acc[h, 0, rows] * SCALE

            def add(src, recv, there):
                term(src, src, 0, h, recv, partner).wait_recv()
                acc[h, :, there] += src[...].astype(jnp.float32)

            for source in range(me + 1, TEAM):
                add(got.at[source - 1, h], gr.at[source - 1, h], rows)
            if me == 0:

                @pl.when(has_left)
                def _():
                    add(got_right.at[h], gh.at[h], pl.ds(OVER, OVER))

            if me == 3:

                @pl.when(has_right)
                def _():
                    add(got.at[1, h], gr.at[1, h], rows)
                    for other in range(TEAM):
                        add(got_left.at[other, h], gl.at[other, h], pl.ds(RIGHT - OVER, OVER))

            for t in range(2):
                columns = pl.ds(pl.multiple_of((t * KVH + h) * HD, HD), HD)
                out[0, :, columns] = acc[h, t, rows].astype(jnp.bfloat16)
            return 0

        lax.fori_loop(0, KVH, finish, 0)

        def drain(h, _):
            for t in range(2):
                to_partner(h, t).wait_send()
                forwards(h, t, lambda copy: copy.wait_send())
            returns(h, lambda copy: copy.wait_send())
            return 0

        lax.fori_loop(0, KVH, drain, 0)
        if me == 0:

            @pl.when(has_left)
            def _():
                for copy in over_queries(at(-2)):
                    copy.wait_send()

        if me % 2 == 0:

            @pl.when(has_left)
            def _():
                tails_on().wait_send()

        if me == 3:

            @pl.when(has_right)
            def _():
                for n in range(2):
                    tails_to(n).wait_send()

    for me in range(TEAM):
        pl.when(j == me)(functools.partial(role, me))


def on_device(n_pipe, n_ctx, queries, stash, grad_out, lengths):
    bf16, f32 = jnp.bfloat16, jnp.float32
    dma = pltpu.SemaphoreType.DMA
    anywhere = pl.BlockSpec(memory_space=pl.ANY)
    return pl.pallas_call(
        functools.partial(kernel, n_pipe, n_ctx),
        out_shape=jax.ShapeDtypeStruct((1, ROWS, 2 * KVH * HD), bf16),
        in_specs=[pl.BlockSpec(memory_space=pltpu.SMEM), anywhere, anywhere, anywhere],
        out_specs=pl.BlockSpec(memory_space=pltpu.VMEM),
        scratch_shapes=[
            pltpu.VMEM((KVH, 2, ROWS, HD), bf16),
            pltpu.VMEM((KVH, 2, SPAN, HD), bf16),
            pltpu.VMEM((H, ROWS, HD), bf16),
            pltpu.VMEM((H, ROWS, HD), bf16),
            pltpu.VMEM((H, OVER, HD), bf16),
            pltpu.VMEM((H, OVER, HD), bf16),
            pltpu.VMEM((KVH, 2, SPAN, HD), f32),
            pltpu.VMEM((KVH, 2, SPAN, HD), bf16),
            pltpu.VMEM((TEAM - 1, KVH, 2, ROWS, HD), bf16),
            pltpu.VMEM((TEAM, KVH, 2, OVER, HD), bf16),
            pltpu.VMEM((KVH, 2, OVER, HD), bf16),
            dma((2 * KVH,)), dma((2,)), dma((2 * KVH,)), dma((2 * KVH,)), dma((4, 2 * KVH)), dma((5, 2 * KVH)),
            dma((2,)), dma((2,)), dma((5, KVH)), dma((3, KVH)), dma((TEAM, KVH)), dma((KVH,)), dma((2,)), dma((2,)),
        ],
        compiler_params=pltpu.CompilerParams(
            collective_id=0, has_side_effects=True, vmem_limit_bytes=67043328,
        ),
        name="document_backward",
    )(lengths, queries, stash, grad_out)


def solution(mesh):
    placed = (P("pipe", "ctx", None), P("pipe", "ctx", None), P("pipe", "ctx", None), P())
    body = functools.partial(on_device, mesh.shape["pipe"], mesh.shape["ctx"])
    return jax.shard_map(body, mesh=mesh, in_specs=placed, out_specs=P("pipe", "ctx", None), check_vma=False)
```
